32 devices in a mesh: gx: 8 (over z, x), ma: 4 (over y, core).
Axes of the slice: x: 2, y: 2, z: 4, core: 2. Of those that a mesh axis runs over, the one named last changes fastest.
Arguments:
- recorded: float32 [4096, 128, 128], P('ma', 'gx'), may hold values from -51 to 51
- kernel: bfloat16 [2, 8, 4096, 4096], P(None, 'gx', 'ma'), may hold values from -1 to 1
- freq_bins: int32 [8], replicated, may hold values from 1 to 63
- window_start: int32 [4096, 128], P('ma', 'gx'), may hold values from 0 to 31
- window_stop: int32 [4096, 128], P('ma', 'gx'), may hold values from 97 to 128
Outputs:
- solution: float32 [4096, 128, 128], P('ma', 'gx')
- residual: float32 [4096, 128, 128], P('ma', 'gx')
- direction: float32 [4096, 128, 128], P('ma', 'gx')
The draws below stay inside these ranges and needn't reach their ends.
All inputs are finite; a program needn't handle non-finite values.
Results may differ from the reference program's by a relative error of at most 0.015.
Values may be sent and summed in bfloat16 or wider, within the bound.
No kernel may reach another device: no remote copies, remote signals or barrier semaphores. Data moves between devices by JAX's collectives and lax.ppermute only.
A program may use at most 128 MiB of HBM per device.

```python
import math
import jax
import jax.numpy as jnp
from jax import lax

NR = 4096
NV = 4096
NT = 128
NS = 128
RAMP = 8
NF = 8


def draw_recorded(key, part):
    key_source = jax.random.fold_in(key, 11)
    key_receiver = jax.random.fold_in(key, 12)
    key_noise = jax.random.fold_in(key, 13)
    key_colour = jax.random.fold_in(key, 15)
    rising = 3.0 ** (jnp.arange(NS, dtype=jnp.float32) / NS)
    source_scale = rising * jnp.exp(jax.random.uniform(key_source, (NS,), jnp.float32) * math.log(10.0))
    receiver_scale = jnp.exp(jax.random.uniform(key_receiver, (NR,), jnp.float32) * math.log(4.0))
    base = jnp.clip(jax.random.normal(key_noise, (NR, NS, NT), jnp.float32), -3.0, 3.0)
    colour = jax.random.uniform(key_colour, (NS,), jnp.float32, -0.9, 0.9)
    delayed = jnp.roll(base, 1, axis=2)
    coloured = (base + colour[None, :, None] * delayed) / jnp.sqrt(1.0 + colour * colour)[None, :, None]
    return 0.1 * coloured * receiver_scale[:, None, None] * source_scale[None, :, None]


def draw_kernel(key, part):
    key_level = jax.random.fold_in(key, 21)
    key_entry = jax.random.fold_in(key, 22)
    level = jnp.exp(jax.random.uniform(key_level, (NF,), jnp.float32, math.log(0.3), math.log(3.0)))
    scale = level[None, :, None, None] / math.sqrt(2.0 * NV)
    entries = jnp.clip(jax.random.normal(key_entry, (2, NF, NR, NV), jnp.float32), -4.0, 4.0)
    return (entries * scale).astype(jnp.bfloat16)


def place_ends(values, own_key, smallest, largest):
    place = [jax.random.randint(jax.random.fold_in(own_key, axis), (), 0, length) for axis, length in enumerate(values.shape)]
    main_axis = values.shape.index(max(values.shape))
    next_to = place[:main_axis] + [(place[main_axis] + 1) % values.shape[main_axis]] + place[main_axis + 1:]
    return values.at[tuple(place)].set(smallest).at[tuple(next_to)].set(largest)


def setup_inputs(seed: int = 0) -> dict:
    keys = jax.random.split(jax.random.key(seed), 6)
    recorded = draw_recorded(jax.random.fold_in(keys[5], 71), 0)
    kernel = draw_kernel(jax.random.fold_in(keys[5], 71), 0)
    freq_bins = place_ends(jax.random.randint(keys[2], (NF,), 1, NT // 2), jax.random.fold_in(keys[2], 1), 1, (NT // 2) - 1).astype(jnp.int32)
    window_start = place_ends(jax.random.randint(keys[3], (NR, NS), 0, NT // 4), jax.random.fold_in(keys[3], 1), 0, (NT // 4) - 1).astype(jnp.int32)
    window_stop = place_ends(jax.random.randint(keys[4], (NR, NS), 3 * NT // 4 + 1, NT + 1), jax.random.fold_in(keys[4], 1), 3 * NT // 4 + 1, NT).astype(jnp.int32)
    return dict(recorded=recorded, kernel=kernel, freq_bins=freq_bins, window_start=window_start, window_stop=window_stop)


epsilon = 1e-06

def phase_table(freq_bins):
    samples = jnp.arange(NT, dtype=jnp.int32)
    angles = (freq_bins[:, None] * samples[None, :] % NT).astype(jnp.float32) * (2.0 * math.pi / NT)
    return jnp.stack([jnp.cos(angles), -jnp.sin(angles)]) * math.sqrt(2.0 / NT)

def taper_weights(window_start, window_stop):
    samples = jnp.arange(NT, dtype=jnp.float32)
    rising = jnp.clip((samples[None, None, :] - window_start[:, :, None].astype(jnp.float32) + 1.0) / RAMP, 0.0, 1.0)
    falling = jnp.clip((window_stop[:, :, None].astype(jnp.float32) - samples[None, None, :]) / RAMP, 0.0, 1.0)
    return rising * falling

def forward_transform(traces, table):
    return jnp.einsum('ast,cft->facs', traces, table, precision=lax.Precision.HIGHEST).astype(jnp.bfloat16)

def inverse_transform(spectra, table):
    return jnp.einsum('facs,cft->ast', spectra.astype(jnp.float32), table, precision=lax.Precision.HIGHEST)

def forward_apply(model_traces, kernel, table, weights):
    spectra = forward_transform(model_traces, table)

    def per_freq(index):
        gains = lax.dynamic_index_in_dim(kernel, index, 1, keepdims=False)
        incoming = lax.dynamic_index_in_dim(spectra, index, 0, keepdims=False)
        real_in = incoming[:, 0, :]
        imag_in = incoming[:, 1, :]
        real_out = jnp.dot(gains[0], real_in, preferred_element_type=jnp.float32) - jnp.dot(gains[1], imag_in, preferred_element_type=jnp.float32)
        imag_out = jnp.dot(gains[0], imag_in, preferred_element_type=jnp.float32) + jnp.dot(gains[1], real_in, preferred_element_type=jnp.float32)
        return jnp.stack([real_out, imag_out], 1).astype(jnp.bfloat16)
    result = lax.map(per_freq, jnp.arange(NF, dtype=jnp.int32))
    return weights * inverse_transform(result, table)

def adjoint_apply(data_traces, kernel, table, weights):
    spectra = forward_transform(weights * data_traces, table)

    def per_freq(index):
        gains = lax.dynamic_index_in_dim(kernel, index, 1, keepdims=False)
        incoming = lax.dynamic_index_in_dim(spectra, index, 0, keepdims=False)
        real_in = incoming[:, 0, :]
        imag_in = incoming[:, 1, :]
        real_out = jnp.dot(gains[0].T, real_in, preferred_element_type=jnp.float32) + jnp.dot(gains[1].T, imag_in, preferred_element_type=jnp.float32)
        imag_out = jnp.dot(gains[0].T, imag_in, preferred_element_type=jnp.float32) - jnp.dot(gains[1].T, real_in, preferred_element_type=jnp.float32)
        return jnp.stack([real_out, imag_out], 1).astype(jnp.bfloat16)
    result = lax.map(per_freq, jnp.arange(NF, dtype=jnp.int32))
    return inverse_transform(result, table)

def reference(recorded, kernel, freq_bins, window_start, window_stop):
    table = phase_table(freq_bins)
    weights = taper_weights(window_start, window_stop)
    gradient = adjoint_apply(recorded, kernel, table, weights)
    norm_start = jnp.sum(gradient * gradient)
    data_image = forward_apply(gradient, kernel, table, weights)
    norm_data = jnp.sum(data_image * data_image)
    step_size = norm_start / (norm_data + epsilon)
    solution = step_size * gradient
    residual = recorded - step_size * data_image
    gradient_new = adjoint_apply(residual, kernel, table, weights)
    norm_final = jnp.sum(gradient_new * gradient_new)
    direction = gradient_new + norm_final / (norm_start + epsilon) * gradient
    return (solution, residual, direction)
```

```python
import functools
import math

import jax
import jax.numpy as jnp
from jax import lax
from jax.experimental import pallas as pl
from jax.experimental.pallas import tpu as pltpu
from jax.sharding import PartitionSpec as P

RAMP = 8

epsilon = 1e-06


bf16 = jnp.bfloat16
f32 = jnp.float32


def phase_rows(freq_bins, length):
    samples = jnp.arange(length, dtype=jnp.int32)
    angles = (freq_bins[:, None] * samples[None, :] % length).astype(f32) * (2.0 * math.pi / length)
    table = jnp.stack([jnp.cos(angles), -jnp.sin(angles)], 1) * math.sqrt(2.0 / length)
    table = table.reshape(2 * freq_bins.shape[0], length)
    high = lax.reduce_precision(table, 8, 7)
    return high.astype(bf16), (table - high).astype(bf16)


def taper(position, rise, fall):
    return jnp.clip(position + rise, 0.0, 1.0) * jnp.clip(fall - position, 0.0, 1.0)


def dot(a, b, ca, cb):
    return lax.dot_general(a, b, (((ca,), (cb,)), ((), ())), preferred_element_type=f32)


def analyse_body(x_ref, rise_ref, fall_ref, tab_ref, out_ref, scr, *, sources, rows):
    block = rise_ref.shape[0]
    length = x_ref.shape[1]
    position = lax.broadcasted_iota(jnp.int32, (block, length), 1).astype(f32) * (1.0 / RAMP)
    for s in range(sources):
        x = x_ref[pl.ds(s, block, stride=sources), :]
        w = taper(position, rise_ref[:, s : s + 1], fall_ref[:, s : s + 1])
        y = dot(tab_ref[...], (x * w).astype(bf16), 1, 1)
        scr[pl.ds(s, rows, stride=sources), :] = y[:rows] + y[rows:]
    out_ref[...] = scr[...].astype(bf16)


def middle_body(y_ref, rise_ref, fall_ref, tab_ref, tabt_ref, out_ref, norm_ref, scr, *, sources, rows):
    block = y_ref.shape[1]
    length = tab_ref.shape[1]
    position = lax.broadcasted_iota(jnp.int32, (length, block), 0).astype(f32) * (1.0 / RAMP)
    scr[...] = y_ref[...].astype(f32)
    total = jnp.zeros((1, block), f32)
    for s in range(sources):
        y = scr[pl.ds(s, rows, stride=sources), :].astype(bf16)
        u = dot(tabt_ref[...], jnp.concatenate([y, y], 0), 1, 0)
        w = taper(position, rise_ref[s : s + 1, :], fall_ref[s : s + 1, :])
        u = u * w
        total += jnp.sum(u * u, axis=0, keepdims=True)
        d = dot(tab_ref[...], (u * w).astype(bf16), 1, 0)
        scr[pl.ds(s, rows, stride=sources), :] = d[:rows] + d[rows:]
    out_ref[...] = scr[...].astype(bf16)
    norm_ref[...] = total


def first_outputs_body(
    step_ref, x_ref, y_ref, z_ref, rise_ref, fall_ref, tab_ref, sol_ref, res_ref, scr_y, scr_z, *, sources, rows
):
    block = rise_ref.shape[0]
    length = x_ref.shape[1]
    step = step_ref[0]
    position = lax.broadcasted_iota(jnp.int32, (block, length), 1).astype(f32) * (1.0 / RAMP)
    scr_y[...] = y_ref[...].astype(f32)
    scr_z[...] = z_ref[...].astype(f32)
    for s in range(sources):
        y = scr_y[pl.ds(s, rows, stride=sources), :].astype(bf16)
        z = scr_z[pl.ds(s, rows, stride=sources), :].astype(bf16)
        u = dot(jnp.concatenate([y, y], 0), tab_ref[...], 0, 0)
        g = dot(jnp.concatenate([z, z], 0), tab_ref[...], 0, 0)
        w = taper(position, rise_ref[:, s : s + 1], fall_ref[:, s : s + 1])
        at = pl.ds(s, block, stride=sources)
        res_ref[at, :] = x_ref[at, :] - step * (w * u)
        sol_ref[at, :] = step * g


def last_output_body(coef_ref, z_ref, q_ref, tab_ref, out_ref, scr, *, sources, rows):
    block = z_ref.shape[1]
    scr[...] = coef_ref[0] * z_ref[...].astype(f32) + coef_ref[1] * q_ref[...].astype(f32)
    for s in range(sources):
        c = scr[pl.ds(s, rows, stride=sources), :]
        high = c.astype(bf16)
        low = (c - high.astype(f32)).astype(bf16)
        out_ref[pl.ds(s, block, stride=sources), :] = dot(
            jnp.concatenate([high, high, low], 0), tab_ref[...], 0, 0
        )


def butterfly(value, axes):
    for axis, size in axes:
        step = 1
        while step < size:
            value = value + lax.ppermute(value, axis, [(i, i ^ step) for i in range(size)])
            step *= 2
    return value


PAIR = [(i, i ^ 1) for i in range(4)]
ACROSS = [(i, i ^ 2) for i in range(4)]


def columns(x, chunk, width):
    return lax.dynamic_slice_in_dim(x, chunk * width, width, 1)


def scatter_sum(x, size):
    width = x.shape[1] // size
    if size != 4:
        return lax.psum_scatter(x, "ma", scatter_dimension=1, tiled=True)
    me = lax.axis_index("ma")
    near = me ^ 1
    far_in = lax.ppermute(columns(x, near ^ 2, width), "ma", PAIR)
    own_in = lax.ppermute(columns(x, near, width), "ma", PAIR)
    far = far_in.astype(f32) + columns(x, me ^ 2, width).astype(f32)
    back = lax.ppermute(far.astype(bf16), "ma", ACROSS)
    return (own_in.astype(f32) + columns(x, me, width).astype(f32) + back.astype(f32)).astype(bf16)


def full_sum(x, size):
    width = x.shape[1] // size
    me = lax.axis_index("ma")
    if size != 4:
        whole = lax.psum(x, "ma")
        return whole, columns(whole, me, width)
    near = me ^ 1
    parts = []
    for flip in (2, 0):
        arrived = lax.ppermute(columns(x, near ^ flip, width), "ma", PAIR)
        parts.append((arrived.astype(f32) + columns(x, me ^ flip, width).astype(f32)).astype(bf16))
    first, second = parts
    from_first = lax.ppermute(first, "ma", ACROSS)
    from_second = lax.ppermute(second, "ma", ACROSS)
    own = (second.astype(f32) + from_first.astype(f32)).astype(bf16)
    other = (first.astype(f32) + from_second.astype(f32)).astype(bf16)
    return spread(own, other), own


def spread(own, other):
    me = lax.axis_index("ma")
    near = me ^ 1
    own_near = lax.ppermute(own, "ma", PAIR)
    other_near = lax.ppermute(other, "ma", PAIR)
    width = own.shape[1]
    whole = jnp.zeros((own.shape[0], 4 * width), own.dtype)
    for block, place in ((own, me), (other, me ^ 2), (own_near, near), (other_near, near ^ 2)):
        whole = lax.dynamic_update_slice_in_dim(whole, block, place * width, 1)
    return whole


def gather(x, size):
    if size != 4:
        return lax.all_gather(x, "ma", axis=1, tiled=True)
    return spread(x, lax.ppermute(x, "ma", ACROSS))


def exchange(x, rows, sources):
    count = lax.axis_size("gx")
    shape = x.shape
    moved = lax.all_to_all(x.reshape(count, shape[0] // count, shape[1]), "gx", 0, 0, tiled=False)
    return moved.reshape(shape)


def per_device(recorded, kernel, freq_bins, window_start, window_stop, *, gx, ma):
    points, sources, length = recorded.shape
    bins = freq_bins.shape[0]
    rows = 2 * bins
    height = rows * sources
    block = min(128, points)
    grid = (points // block,)
    flat_kernel = kernel.reshape(2 * kernel.shape[2], kernel.shape[3])
    traces = recorded.reshape(points * sources, length)

    high, low = phase_rows(freq_bins, length)
    forward_rows = jnp.concatenate([high, low], 0)
    inverse_rows = jnp.concatenate([high, low, high], 0)
    rise = (1.0 - window_start.astype(f32)) * (1.0 / RAMP)
    fall = window_stop.astype(f32) * (1.0 / RAMP)

    equal = freq_bins[:, None] == freq_bins[None, :]
    distinct = jnp.sum(equal.astype(jnp.int32)) == bins
    mixing = jnp.kron(equal.astype(bf16), jnp.eye(2 * sources, dtype=bf16))

    trace_spec = pl.BlockSpec((block * sources, length), lambda i: (i, 0))
    spectra_spec = pl.BlockSpec((height, block), lambda i: (0, i))
    window_spec = pl.BlockSpec((block, sources), lambda i: (i, 0))
    window_t_spec = pl.BlockSpec((sources, block), lambda i: (0, i))
    whole = lambda a: pl.BlockSpec(a.shape, lambda i: (0, 0))
    scalar_spec = pl.BlockSpec(memory_space=pltpu.SMEM)
    spectra_shape = jax.ShapeDtypeStruct((height, points), bf16)
    trace_shape = jax.ShapeDtypeStruct(traces.shape, f32)
    scratch = pltpu.VMEM((height, block), f32)
    fixed = dict(sources=sources, rows=rows)

    sent = pl.pallas_call(
        functools.partial(analyse_body, **fixed),
        grid=grid,
        in_specs=[trace_spec, window_spec, window_spec, whole(forward_rows)],
        out_specs=spectra_spec,
        out_shape=spectra_shape,
        scratch_shapes=[scratch],
        name="analyse",
    )(traces, rise, fall, forward_rows)

    def adjoint_product(spectra):
        x = exchange(spectra, rows, sources)
        x4 = x.reshape(gx, 2, sources, points)
        turned = jnp.stack([x4[:, 1], -x4[:, 0]], 1).reshape(height, points)
        return dot(jnp.concatenate([x, turned], 1), flat_kernel, 1, 0).astype(bf16)

    product = adjoint_product(sent)
    summed, own = full_sum(product, ma)

    def mixed(own_block):
        there = exchange(own_block, rows, sources)
        back = exchange(dot(mixing, there, 1, 0).astype(bf16), rows, sources)
        return gather(back, ma)

    incoming = lax.cond(distinct, lambda s, o: s, lambda s, o: mixed(o), summed, own)
    forward = dot(incoming, flat_kernel, 1, 1).reshape(gx, 2, sources, 2 * points)
    upper, lower = forward[..., :points], forward[..., points:]
    outgoing = jnp.stack([upper[:, 0] - lower[:, 1], upper[:, 1] + lower[:, 0]], 1)
    image = exchange(outgoing.astype(bf16).reshape(height, points), rows, sources)

    second, norm_rows = pl.pallas_call(
        functools.partial(middle_body, **fixed),
        grid=grid,
        in_specs=[spectra_spec, window_t_spec, window_t_spec, whole(forward_rows), whole(forward_rows.T)],
        out_specs=[spectra_spec, pl.BlockSpec((1, block), lambda i: (0, i))],
        out_shape=[spectra_shape, jax.ShapeDtypeStruct((1, points), f32)],
        scratch_shapes=[scratch],
        name="middle",
    )(image, rise.T, fall.T, forward_rows, forward_rows.T)

    first = exchange(own, rows, sources)
    first_f32 = first.astype(f32)
    axes = (("ma", ma), ("gx", gx))
    early = butterfly(
        jnp.stack([jnp.sum(first_f32 * dot(mixing, first, 1, 0)), jnp.sum(norm_rows)]), axes
    )
    norm_start = early[0]
    step_size = norm_start / (early[1] + epsilon)

    change = exchange(scatter_sum(adjoint_product(second), ma), rows, sources)
    change_mixed = dot(mixing, change, 1, 0)
    late = butterfly(
        jnp.stack([jnp.sum(first_f32 * change_mixed), jnp.sum(change.astype(f32) * change_mixed)]), axes
    )

    solution_traces, residual = pl.pallas_call(
        functools.partial(first_outputs_body, **fixed),
        grid=grid,
        in_specs=[
            scalar_spec, trace_spec, spectra_spec, spectra_spec, window_spec, window_spec, whole(forward_rows)
        ],
        out_specs=[trace_spec, trace_spec],
        out_shape=[trace_shape, trace_shape],
        scratch_shapes=[scratch, scratch],
        name="outputs",
    )(step_size[None], traces, image, first, rise, fall, forward_rows)

    norm_final = norm_start - 2.0 * step_size * late[0] + step_size * step_size * late[1]
    ratio = norm_final / (norm_start + epsilon)
    direction = pl.pallas_call(
        functools.partial(last_output_body, **fixed),
        grid=grid,
        in_specs=[scalar_spec, spectra_spec, spectra_spec, whole(inverse_rows)],
        out_specs=trace_spec,
        out_shape=trace_shape,
        scratch_shapes=[scratch],
        name="direction",
    )(jnp.stack([1.0 + ratio, -step_size]), first, change, inverse_rows)

    shape = recorded.shape
    return solution_traces.reshape(shape), residual.reshape(shape), direction.reshape(shape)


def solution(mesh):
    in_specs = (P("ma", "gx", None), P(None, "gx", "ma", None), P(), P("ma", "gx"), P("ma", "gx"))
    out_specs = (P("ma", "gx", None), P("ma", "gx", None), P("ma", "gx", None))
    body = functools.partial(per_device, gx=mesh.shape["gx"], ma=mesh.shape["ma"])
    return jax.shard_map(body, mesh=mesh, in_specs=in_specs, out_specs=out_specs, check_vma=False)
```

```python
import functools
import math

import jax
import jax.numpy as jnp
from jax import lax
from jax.experimental import pallas as pl
from jax.experimental.pallas import tpu as pltpu
from jax.sharding import PartitionSpec as P

RAMP = 8

epsilon = 1e-06


bf16 = jnp.bfloat16
f32 = jnp.float32


def phase_rows(freq_bins, length):
    samples = jnp.arange(length, dtype=jnp.int32)
    angles = (freq_bins[:, None] * samples[None, :] % length).astype(f32) * (2.0 * math.pi / length)
    table = jnp.stack([jnp.cos(angles), -jnp.sin(angles)], 1) * math.sqrt(2.0 / length)
    table = table.reshape(2 * freq_bins.shape[0], length)
    high = lax.reduce_precision(table, 8, 7)
    return high.astype(bf16), (table - high).astype(bf16)


def taper(position, rise, fall):
    return jnp.clip(position + rise, 0.0, 1.0) * jnp.clip(fall - position, 0.0, 1.0)


def dot(a, b, ca, cb):
    return lax.dot_general(a, b, (((ca,), (cb,)), ((), ())), preferred_element_type=f32)


def analyse_body(x_ref, rise_ref, fall_ref, tab_ref, out_ref, scr, *, sources, rows):
    block = rise_ref.shape[0]
    length = x_ref.shape[1]
    position = lax.broadcasted_iota(jnp.int32, (block, length), 1).astype(f32) * (1.0 / RAMP)
    for s in range(sources):
        x = x_ref[pl.ds(s, block, stride=sources), :]
        w = taper(position, rise_ref[:, s : s + 1], fall_ref[:, s : s + 1])
        y = dot(tab_ref[...], (x * w).astype(bf16), 1, 1)
        scr[pl.ds(s, rows, stride=sources), :] = y[:rows] + y[rows:]
    out_ref[...] = scr[...].astype(bf16)


def middle_body(y_ref, rise_ref, fall_ref, tab_ref, tabt_ref, out_ref, norm_ref, scr, *, sources, rows):
    block = y_ref.shape[1]
    length = tab_ref.shape[1]
    position = lax.broadcasted_iota(jnp.int32, (length, block), 0).astype(f32) * (1.0 / RAMP)
    scr[...] = y_ref[...].astype(f32)
    total = jnp.zeros((1, block), f32)
    for s in range(sources):
        y = scr[pl.ds(s, rows, stride=sources), :].astype(bf16)
        u = dot(tabt_ref[...], jnp.concatenate([y, y], 0), 1, 0)
        w = taper(position, rise_ref[s : s + 1, :], fall_ref[s : s + 1, :])
        u = u * w
        total += jnp.sum(u * u, axis=0, keepdims=True)
        d = dot(tab_ref[...], (u * w).astype(bf16), 1, 0)
        scr[pl.ds(s, rows, stride=sources), :] = d[:rows] + d[rows:]
    out_ref[...] = scr[...].astype(bf16)
    norm_ref[...] = total


def first_outputs_body(
    step_ref, x_ref, y_ref, z_ref, rise_ref, fall_ref, tab_ref, sol_ref, res_ref, scr_y, scr_z, *, sources, rows
):
    block = rise_ref.shape[0]
    length = x_ref.shape[1]
    step = step_ref[0]
    position = lax.broadcasted_iota(jnp.int32, (block, length), 1).astype(f32) * (1.0 / RAMP)
    scr_y[...] = y_ref[...].astype(f32)
    scr_z[...] = z_ref[...].astype(f32)
    for s in range(sources):
        y = scr_y[pl.ds(s, rows, stride=sources), :].astype(bf16)
        z = scr_z[pl.ds(s, rows, stride=sources), :].astype(bf16)
        u = dot(jnp.concatenate([y, y], 0), tab_ref[...], 0, 0)
        g = dot(jnp.concatenate([z, z], 0), tab_ref[...], 0, 0)
        w = taper(position, rise_ref[:, s : s + 1], fall_ref[:, s : s + 1])
        at = pl.ds(s, block, stride=sources)
        res_ref[at, :] = x_ref[at, :] - step * (w * u)
        sol_ref[at, :] = step * g


def last_output_body(coef_ref, z_ref, q_ref, tab_ref, out_ref, scr, *, sources, rows):
    block = z_ref.shape[1]
    scr[...] = coef_ref[0] * z_ref[...].astype(f32) + coef_ref[1] * q_ref[...].astype(f32)
    for s in range(sources):
        c = scr[pl.ds(s, rows, stride=sources), :]
        high = c.astype(bf16)
        low = (c - high.astype(f32)).astype(bf16)
        out_ref[pl.ds(s, block, stride=sources), :] = dot(
            jnp.concatenate([high, high, low], 0), tab_ref[...], 0, 0
        )


def butterfly(value, axes):
    for axis, size in axes:
        step = 1
        while step < size:
            value = value + lax.ppermute(value, axis, [(i, i ^ step) for i in range(size)])
            step *= 2
    return value


PAIR = [(i, i ^ 1) for i in range(4)]
ACROSS = [(i, i ^ 2) for i in range(4)]


def columns(x, chunk, width):
    return lax.dynamic_slice_in_dim(x, chunk * width, width, 1)


def scatter_sum(x, size):
    width = x.shape[1] // size
    if size != 4:
        return lax.psum_scatter(x, "ma", scatter_dimension=1, tiled=True)
    me = lax.axis_index("ma")
    near = me ^ 1
    far_in = lax.ppermute(columns(x, near ^ 2, width), "ma", PAIR)
    own_in = lax.ppermute(columns(x, near, width), "ma", PAIR)
    far = far_in.astype(f32) + columns(x, me ^ 2, width).astype(f32)
    back = lax.ppermute(far.astype(bf16), "ma", ACROSS)
    return (own_in.astype(f32) + columns(x, me, width).astype(f32) + back.astype(f32)).astype(bf16)


def full_sum(x, size):
    width = x.shape[1] // size
    me = lax.axis_index("ma")
    if size != 4:
        whole = lax.psum(x, "ma")
        return (whole,), columns(whole, me, width)
    near = me ^ 1
    parts = []
    for flip in (2, 0):
        arrived = lax.ppermute(columns(x, near ^ flip, width), "ma", PAIR)
        parts.append((arrived.astype(f32) + columns(x, me ^ flip, width).astype(f32)).astype(bf16))
    first, second = parts
    from_first = lax.ppermute(first, "ma", ACROSS)
    from_second = lax.ppermute(second, "ma", ACROSS)
    own = (second.astype(f32) + from_first.astype(f32)).astype(bf16)
    other = (first.astype(f32) + from_second.astype(f32)).astype(bf16)
    return spread(own, other), own


def spread(own, other):
    me = lax.axis_index("ma")
    near = me ^ 1
    own_near = lax.ppermute(own, "ma", PAIR)
    other_near = lax.ppermute(other, "ma", PAIR)
    return own, other, own_near, other_near


def assemble(own, other, own_near, other_near):
    me = lax.axis_index("ma")
    odd, upper = me % 2 == 1, me >= 2
    here = (jnp.where(odd, own_near, own), jnp.where(odd, own, own_near))
    there = (jnp.where(odd, other_near, other), jnp.where(odd, other, other_near))
    return jnp.concatenate(
        [jnp.where(upper, t, h) for h, t in zip(here, there)]
        + [jnp.where(upper, h, t) for h, t in zip(here, there)], 1
    )


def gather(x, size):
    if size != 4:
        return (lax.all_gather(x, "ma", axis=1, tiled=True),)
    return spread(x, lax.ppermute(x, "ma", ACROSS))


def exchange(x, rows, sources):
    count = lax.axis_size("gx")
    shape = x.shape
    moved = lax.all_to_all(x.reshape(count, shape[0] // count, shape[1]), "gx", 0, 0, tiled=False)
    return moved.reshape(shape)


def per_device(recorded, kernel, freq_bins, window_start, window_stop, *, gx, ma):
    points, sources, length = recorded.shape
    bins = freq_bins.shape[0]
    rows = 2 * bins
    height = rows * sources
    block = min(128, points)
    grid = (points // block,)
    flat_kernel = kernel.reshape(2 * kernel.shape[2], kernel.shape[3])
    traces = recorded.reshape(points * sources, length)

    high, low = phase_rows(freq_bins, length)
    forward_rows = jnp.concatenate([high, low], 0)
    inverse_rows = jnp.concatenate([high, low, high], 0)
    rise = (1.0 - window_start.astype(f32)) * (1.0 / RAMP)
    fall = window_stop.astype(f32) * (1.0 / RAMP)

    equal = freq_bins[:, None] == freq_bins[None, :]
    distinct = jnp.sum(equal.astype(jnp.int32)) == bins
    mixing = jnp.kron(equal.astype(bf16), jnp.eye(2 * sources, dtype=bf16))

    trace_spec = pl.BlockSpec((block * sources, length), lambda i: (i, 0))
    spectra_spec = pl.BlockSpec((height, block), lambda i: (0, i))
    window_spec = pl.BlockSpec((block, sources), lambda i: (i, 0))
    window_t_spec = pl.BlockSpec((sources, block), lambda i: (0, i))
    whole = lambda a: pl.BlockSpec(a.shape, lambda i: (0, 0))
    scalar_spec = pl.BlockSpec(memory_space=pltpu.SMEM)
    spectra_shape = jax.ShapeDtypeStruct((height, points), bf16)
    trace_shape = jax.ShapeDtypeStruct(traces.shape, f32)
    scratch = pltpu.VMEM((height, block), f32)
    fixed = dict(sources=sources, rows=rows)

    sent = pl.pallas_call(
        functools.partial(analyse_body, **fixed),
        grid=grid,
        in_specs=[trace_spec, window_spec, window_spec, whole(forward_rows)],
        out_specs=spectra_spec,
        out_shape=spectra_shape,
        scratch_shapes=[scratch],
        name="analyse",
    )(traces, rise, fall, forward_rows)

    def adjoint_product(spectra):
        x = exchange(spectra, rows, sources)
        x4 = x.reshape(gx, 2, sources, points)
        turned = jnp.stack([x4[:, 1], -x4[:, 0]], 1).reshape(height, points)
        return dot(jnp.concatenate([x, turned], 1), flat_kernel, 1, 0).astype(bf16)

    product = adjoint_product(sent)
    summed, own = full_sum(product, ma)

    def mixed(own_block):
        there = exchange(own_block, rows, sources)
        back = exchange(dot(mixing, there, 1, 0).astype(bf16), rows, sources)
        return gather(back, ma)

    incoming = lax.cond(distinct, lambda s, o: s, lambda s, o: mixed(o), summed, own)
    incoming = assemble(*incoming) if len(incoming) == 4 else incoming[0]
    forward = dot(incoming, flat_kernel, 1, 1).reshape(gx, 2, sources, 2 * points)
    upper, lower = forward[..., :points], forward[..., points:]
    outgoing = jnp.stack([upper[:, 0] - lower[:, 1], upper[:, 1] + lower[:, 0]], 1)
    image = exchange(outgoing.astype(bf16).reshape(height, points), rows, sources)

    second, norm_rows = pl.pallas_call(
        functools.partial(middle_body, **fixed),
        grid=grid,
        in_specs=[spectra_spec, window_t_spec, window_t_spec, whole(forward_rows), whole(forward_rows.T)],
        out_specs=[spectra_spec, pl.BlockSpec((1, block), lambda i: (0, i))],
        out_shape=[spectra_shape, jax.ShapeDtypeStruct((1, points), f32)],
        scratch_shapes=[scratch],
        name="middle",
    )(image, rise.T, fall.T, forward_rows, forward_rows.T)

    first = exchange(own, rows, sources)
    first_f32 = first.astype(f32)
    axes = (("ma", ma), ("gx", gx))
    change = exchange(scatter_sum(adjoint_product(second), ma), rows, sources)
    change_mixed = dot(mixing, change, 1, 0)
    sums = butterfly(
        jnp.stack(
            [
                jnp.sum(first_f32 * dot(mixing, first, 1, 0)),
                jnp.sum(norm_rows),
                jnp.sum(first_f32 * change_mixed),
                jnp.sum(change.astype(f32) * change_mixed),
            ]
        ),
        (("ma", ma), ("gx", gx)),
    )
    norm_start = sums[0]
    step_size = norm_start / (sums[1] + epsilon)

    solution_traces, residual = pl.pallas_call(
        functools.partial(first_outputs_body, **fixed),
        grid=grid,
        in_specs=[
            scalar_spec, trace_spec, spectra_spec, spectra_spec, window_spec, window_spec, whole(forward_rows)
        ],
        out_specs=[trace_spec, trace_spec],
        out_shape=[trace_shape, trace_shape],
        scratch_shapes=[scratch, scratch],
        name="outputs",
    )(step_size[None], traces, image, first, rise, fall, forward_rows)

    norm_final = norm_start - 2.0 * step_size * sums[2] + step_size * step_size * sums[3]
    ratio = norm_final / (norm_start + epsilon)
    direction = pl.pallas_call(
        functools.partial(last_output_body, **fixed),
        grid=grid,
        in_specs=[scalar_spec, spectra_spec, spectra_spec, whole(inverse_rows)],
        out_specs=trace_spec,
        out_shape=trace_shape,
        scratch_shapes=[scratch],
        name="direction",
    )(jnp.stack([1.0 + ratio, -step_size]), first, change, inverse_rows)

    shape = recorded.shape
    return solution_traces.reshape(shape), residual.reshape(shape), direction.reshape(shape)


def solution(mesh):
    in_specs = (P("ma", "gx", None), P(None, "gx", "ma", None), P(), P("ma", "gx"), P("ma", "gx"))
    out_specs = (P("ma", "gx", None), P("ma", "gx", None), P("ma", "gx", None))
    body = functools.partial(per_device, gx=mesh.shape["gx"], ma=mesh.shape["ma"])
    return jax.shard_map(body, mesh=mesh, in_specs=in_specs, out_specs=out_specs, check_vma=False)
```
